32 devices in a mesh: grp: 4 (over y, x), leaf: 8 (over z, core).
Axes of the slice: x: 2, y: 2, z: 4, core: 2. Of those that a mesh axis runs over, the one named last changes fastest.
Arguments:
- right_side: float32 [24576, 512], P(('grp', 'leaf')), may hold values from -6 to 6
- guess: float32 [24576, 512], P(('grp', 'leaf')), may hold values from -6 to 6
- near_diag: float32 [32, 768, 768], P(('grp', 'leaf')), as said below
- near_lower: float32 [32, 768, 768], P(('grp', 'leaf')), may hold values from -0.0546875 to 0.0546875
- near_upper: float32 [32, 768, 768], P(('grp', 'leaf')), may hold values from -0.0546875 to 0.0546875
- leaf_inverse: float32 [32, 768, 768], P(('grp', 'leaf')), as said below
- leaf_basis: float32 [32, 768, 128], P(('grp', 'leaf')), may hold values from -0.21875 to 0.21875
- leaf_transfer: float32 [32, 128, 128], P(('grp', 'leaf')), may hold values from -0.5 to 0.5
- mid_share: float32 [32, 128, 128], P(('grp', 'leaf')), may hold values from -0.25 to 0.25
- top_share: float32 [32, 128, 128], P(('grp', 'leaf')), may hold values from -0.1875 to 0.1875
- coupling_share: float32 [32, 3, 128, 128], P(('grp', 'leaf')), as said below
Outputs:
- new_guess: float32 [24576, 512], P(('grp', 'leaf'))
- new_residual: float32 [24576, 512], P(('grp', 'leaf'))
The draws below stay inside these ranges and needn't reach their ends.
Inputs may be any that keep to these rules, and one draw needn't show every extreme that they name: `near_diag`: each leaf's block has a dominant diagonal near 2. `leaf_inverse`: each leaf's matrix is symmetric positive definite. `coupling_share`: every share is symmetric, and each sum of shares that forms a coupling is positive definite.
All inputs are finite; a program needn't handle non-finite values.
Results may differ from the reference program's by a relative error of at most 0.00005.
Values sent between devices are 32-bit elements; how exact they have to be, the bound alone decides.
No kernel may reach another device: no remote copies, remote signals or barrier semaphores. Data moves between devices by JAX's collectives and lax.ppermute only.
A program may use at most 128 MiB of HBM per device.

```python
import math
import jax
import jax.numpy as jnp
from jax import lax

LEAF = 768
RANK = 128
RHS = 512
PER_GROUP = 8
LEAVES = 32
ORDER = 24576


def draw_near_diag(key, part):
    own_key = jax.random.fold_in(key, 11)
    noise = jax.random.normal(own_key, (LEAVES, LEAF, LEAF), jnp.float32)
    return 2.0 * jnp.eye(LEAF, dtype=jnp.float32) + noise * (0.5 / math.sqrt(LEAF))


def draw_leaf_inverse(key, part):
    own_key = jax.random.fold_in(key, 23)
    noise = jax.random.normal(own_key, (LEAVES, LEAF, LEAF), jnp.float32)
    symmetric = (noise + jnp.swapaxes(noise, 1, 2)) * (0.25 / math.sqrt(2.0 * LEAF))
    return jnp.eye(LEAF, dtype=jnp.float32) + symmetric


def draw_coupling_share(key, part):
    own_key = jax.random.fold_in(key, 37)
    noise = jax.random.normal(own_key, (LEAVES, 3, RANK, RANK), jnp.float32)
    symmetric = (noise + jnp.swapaxes(noise, 2, 3)) * (0.3 / math.sqrt(2.0 * RANK))
    counts = jnp.array([4.0, PER_GROUP * 1.0, LEAVES * 1.0], jnp.float32).reshape(1, 3, 1, 1)
    return jnp.eye(RANK, dtype=jnp.float32) / counts + symmetric / jnp.sqrt(counts)


def shard_levels(key, shape, split, low, top_value):
    loudness = 1.0
    for dim, shards_of in split:
        heights = jax.random.uniform(jax.random.fold_in(jax.random.fold_in(key, 6), dim), (shards_of,), jnp.float32, low / len(split), top_value / len(split))
        loudness = loudness * jnp.repeat(jnp.exp(heights), shape[dim] // shards_of).reshape((-1,) + (1,) * (len(shape) - 1 - dim))
    return loudness


def gaussian(key, shape, width, bound, split=(), held_as=jnp.bfloat16):
    values = width * jax.random.normal(key, shape, jnp.float32)
    if split:
        values = values * shard_levels(key, shape, split, -0.22, 0.18)
    return jnp.clip(values, -bound, bound).astype(held_as)


def setup_inputs(seed: int = 0) -> dict:
    arg_keys = jax.random.split(jax.random.key(seed), 12)
    right_side = gaussian(arg_keys[0], (ORDER, RHS), 1.0, 6.0, ((0, 32),), jnp.float32)
    guess = gaussian(arg_keys[1], (ORDER, RHS), 1.0, 6.0, ((0, 32),), jnp.float32)
    near_diag = draw_near_diag(jax.random.fold_in(arg_keys[11], 71), 0)
    near_lower = gaussian(arg_keys[3], (LEAVES, LEAF, LEAF), (16 * LEAF) ** -0.5, 0.0546875, ((0, 32),), jnp.float32)
    near_upper = gaussian(arg_keys[4], (LEAVES, LEAF, LEAF), (16 * LEAF) ** -0.5, 0.0546875, ((0, 32),), jnp.float32)
    leaf_inverse = draw_leaf_inverse(jax.random.fold_in(arg_keys[11], 71), 0)
    leaf_basis = gaussian(arg_keys[6], (LEAVES, LEAF, RANK), LEAF ** -0.5, 0.21875, ((0, 32),), jnp.float32)
    leaf_transfer = gaussian(arg_keys[7], (LEAVES, RANK, RANK), RANK ** -0.5, 0.5, ((0, 32),), jnp.float32)
    mid_share = gaussian(arg_keys[8], (LEAVES, RANK, RANK), (4 * RANK) ** -0.5, 0.25, ((0, 32),), jnp.float32)
    top_share = gaussian(arg_keys[9], (LEAVES, RANK, RANK), (PER_GROUP * RANK) ** -0.5, 0.1875, ((0, 32),), jnp.float32)
    coupling_share = draw_coupling_share(jax.random.fold_in(arg_keys[11], 71), 0)
    return {"right_side": right_side, "guess": guess, "near_diag": near_diag, "near_lower": near_lower, "near_upper": near_upper, "leaf_inverse": leaf_inverse, "leaf_basis": leaf_basis, "leaf_transfer": leaf_transfer, "mid_share": mid_share, "top_share": top_share, "coupling_share": coupling_share}


highest = lax.Precision.HIGHEST

def product(left, right):
    return jnp.einsum('...kl,...lr->...kr', left, right, precision=highest)

def across(left, right):
    return jnp.einsum('...kl,...kr->...lr', left, right, precision=highest)

def definite_solve(matrix, target):
    factor = jnp.linalg.cholesky(matrix)
    halfway = lax.linalg.triangular_solve(factor, target, left_side=True, lower=True)
    return lax.linalg.triangular_solve(factor, halfway, left_side=True, lower=True, transpose_a=True)

def near_apply(blocks, near_diag, near_lower, near_upper):
    zero_block = jnp.zeros_like(blocks[:1])
    below_blocks = jnp.concatenate([zero_block, blocks[:-1]], 0)
    above_blocks = jnp.concatenate([blocks[1:], zero_block], 0)
    result = product(near_diag, blocks)
    result = result + product(near_lower, below_blocks)
    return result + product(near_upper, above_blocks)

def by_count(values, group_size):
    return values.reshape((values.shape[0] // group_size, group_size) + values.shape[1:]).sum(1)

def reference(right_side, guess, near_diag, near_lower, near_upper, leaf_inverse, leaf_basis, leaf_transfer, mid_share, top_share, coupling_share):
    blocks_b = right_side.reshape(LEAVES, LEAF, RHS)
    start_x = guess.reshape(LEAVES, LEAF, RHS)
    residual = blocks_b - near_apply(start_x, near_diag, near_lower, near_upper)
    weighted = product(leaf_inverse, leaf_basis)
    leaf_schur = across(leaf_basis, weighted)
    local_sol = product(leaf_inverse, residual)
    reduced = across(leaf_basis, local_sol)
    block_rhs = by_count(across(leaf_transfer, reduced), 4)
    block_proj = by_count(across(leaf_transfer, product(leaf_schur, leaf_transfer)), 4)
    block_mid = by_count(mid_share, 4)
    block_sys = by_count(coupling_share[:, 0], 4) + block_proj
    block_schur = block_proj - product(block_proj, definite_solve(block_sys, block_proj))
    block_red = block_rhs - product(block_proj, definite_solve(block_sys, block_rhs))
    node_count = PER_GROUP // 4
    group_rhs = by_count(across(block_mid, block_red), node_count)
    group_proj = by_count(across(block_mid, product(block_schur, block_mid)), node_count)
    group_top = by_count(top_share, PER_GROUP)
    group_sys = by_count(coupling_share[:, 1], PER_GROUP) + group_proj
    group_schur = group_proj - product(group_proj, definite_solve(group_sys, group_proj))
    group_red = group_rhs - product(group_proj, definite_solve(group_sys, group_rhs))
    root_rhs = across(group_top, group_red).sum(0)
    root_proj = across(group_top, product(group_schur, group_top)).sum(0)
    root_sys = coupling_share[:, 2].sum(0) + root_proj
    root_t = definite_solve(root_sys, root_rhs)
    group_in = product(group_top, root_t[None])
    group_out = group_in + definite_solve(group_sys, group_rhs - product(group_proj, group_in))
    block_in = product(block_mid, jnp.repeat(group_out, node_count, 0))
    block_out = block_in + definite_solve(block_sys, block_rhs - product(block_proj, block_in))
    leaf_in = product(leaf_transfer, jnp.repeat(block_out, 4, 0))
    new_blocks = start_x + (local_sol - product(weighted, leaf_in))
    new_resid = blocks_b - near_apply(new_blocks, near_diag, near_lower, near_upper)
    return (new_blocks.reshape(ORDER, RHS), new_resid.reshape(ORDER, RHS))
```

```python
import functools

import jax
import jax.numpy as jnp
from jax import lax
from jax.experimental import pallas as pl
from jax.experimental.pallas import tpu as pltpu
from jax.sharding import PartitionSpec as P

highest = lax.Precision.HIGHEST
NODE = 4
ROWS = 256
AXES = ("grp", "leaf")
f32, bf16 = jnp.float32, jnp.bfloat16


def exact(left, right):
    return jnp.dot(left, right, precision=highest, preferred_element_type=f32)


def exact_across(left, right):
    return lax.dot_general(
        left, right, (((0,), (0,)), ((), ())), precision=highest, preferred_element_type=f32
    )


def split(value):
    high = value.astype(bf16)
    return high, (value - high.astype(f32)).astype(bf16)


def mul(left, right):
    dims = (((1,), (0,)), ((), ()))
    dot = functools.partial(lax.dot_general, dimension_numbers=dims, preferred_element_type=f32)
    return dot(left[0], right[0]) + (dot(left[0], right[1]) + dot(left[1], right[0]))


def mul_across(left, right):
    dims = (((0,), (0,)), ((), ()))
    dot = functools.partial(lax.dot_general, dimension_numbers=dims, preferred_element_type=f32)
    return dot(left[0], right[0]) + (dot(left[0], right[1]) + dot(left[1], right[0]))


def inverse(matrix):
    size = matrix.shape[0]
    width, tile = 4, 8
    count = size // tile
    lane = lax.broadcasted_iota(jnp.int32, (tile, size), 1)
    row = lax.broadcasted_iota(jnp.int32, (tile, size), 0)

    def spread(value):
        return jnp.broadcast_to(value, (tile, size))

    def eliminate(tiles, first):
        pivots = range(width)
        columns = [spread(tiles[0][:, first + j : first + j + 1]) for j in pivots]
        corner = [[spread(columns[j][first + i : first + i + 1, :]) for j in pivots] for i in pivots]
        inside = (lane >= first) & (lane < first + width)
        rows = [
            jnp.where(
                inside,
                jnp.where(lane == first + i, 1.0, 0.0),
                spread(tiles[0][first + i : first + i + 1, :]),
            )
            for i in pivots
        ]
        for p in pivots:
            scale = 1.0 / corner[p][p]
            rows[p] = rows[p] * scale
            for q in range(p + 1, width):
                corner[p][q] = corner[p][q] * scale
            for i in pivots:
                if i != p:
                    factor = corner[i][p]
                    rows[i] = rows[i] - factor * rows[p]
                    for q in range(p + 1, width):
                        corner[i][q] = corner[i][q] - factor * corner[p][q]
        out = []
        for t in range(count):
            left = columns
            if t:
                left = [spread(tiles[t][:, first + j : first + j + 1]) for j in pivots]
            value = jnp.where(inside, 0.0, tiles[t])
            for j in pivots:
                value = value - left[j] * rows[j]
            if t == 0:
                for i in pivots:
                    value = jnp.where(row == first + i, rows[i], value)
            out.append(value)
        return out

    def step(_, tiles):
        tiles = list(tiles)
        for first in range(0, tile, width):
            tiles = eliminate(tiles, first)
        tiles = [pltpu.roll(value, size - tile, 1) for value in tiles]
        return tuple(tiles[1:] + tiles[:1])

    tiles = tuple(matrix[tile * t : tile * (t + 1)] for t in range(count))
    return jnp.concatenate(lax.fori_loop(0, count, step, tiles), 0)


def call(kernel, flags, operands, specs, outs, out_specs, grid=(1,), scratch=(), flops=0):
    moved = sum(4 * value.size for value in operands) + sum(4 * out.size for out in outs)
    return pl.pallas_call(
        kernel,
        out_shape=outs,
        grid_spec=pltpu.PrefetchScalarGridSpec(
            num_scalar_prefetch=1,
            grid=grid,
            in_specs=specs,
            out_specs=out_specs,
            scratch_shapes=list(scratch),
        ),
        cost_estimate=pl.CostEstimate(flops=flops, bytes_accessed=moved, transcendentals=0),
    )(flags, *operands)


def whole(shape):
    return pl.BlockSpec(shape, lambda s, f: (0,) * len(shape))


def small(kernel, flags, operands, shapes, flops=0):
    outs = [jax.ShapeDtypeStruct(shape, f32) for shape in shapes]
    return call(
        kernel,
        flags,
        operands,
        [whole(value.shape) for value in operands],
        outs,
        [whole(shape) for shape in shapes],
        flops=flops,
    )


def strip(columns):
    return pl.BlockSpec((ROWS, columns), lambda s, f: (s, 0))


def leaf_setup(flags, inverse_block, basis, transfer, mid, top, shares):
    rows, rank = basis.shape

    def kernel(f, a, b, t, m, p, c, stack, weight, leaf):
        step = pl.program_id(0)

        @pl.when(step == 0)
        def _():
            leaf[...] = exact(b[...], t[...])
            stack[pl.ds(rows, rank), :] = jnp.zeros((rank, rank), f32)
            stack[pl.ds(rows + rank, rank), :] = c[0]
            stack[pl.ds(rows + 2 * rank, rank), :] = m[...]
            stack[pl.ds(rows + 3 * rank, rank), :] = c[1]
            stack[pl.ds(rows + 4 * rank, rank), :] = p[...]
            stack[pl.ds(rows + 5 * rank, rank), :] = c[2]

        at = pl.multiple_of(step * ROWS, ROWS)
        value = exact(a[...], leaf[...])
        stack[pl.ds(at, ROWS), :] = value
        weight[...] = value
        stack[pl.ds(rows, rank), :] += exact_across(leaf[pl.ds(at, ROWS), :], value)

    full = rows + 6 * rank
    return call(
        kernel,
        flags,
        (inverse_block, basis, transfer, mid, top, shares),
        [
            strip(rows),
            whole((rows, rank)),
            whole((rank, rank)),
            whole((rank, rank)),
            whole((rank, rank)),
            whole((3, rank, rank)),
        ],
        [jax.ShapeDtypeStruct((full, rank), f32), jax.ShapeDtypeStruct((rows, rank), f32)],
        [whole((full, rank)), strip(rank)],
        grid=(rows // ROWS,),
        scratch=[pltpu.VMEM((rows, rank), f32)],
        flops=6 * 2 * rows * rows * rank,
    )


def block_matrices(flags, own, other):
    rank = own.shape[1]

    def kernel(f, x, y, sys_inverse, down, rest):
        part = [x[pl.ds(k * rank, rank), :] + y[pl.ds(k * rank, rank), :] for k in range(6)]
        proj, coup, mid = part[:3]
        inv = inverse(proj + coup)
        sys_inverse[...] = inv
        lower = exact(exact(inv, coup), mid)
        down[...] = lower
        rest[pl.ds(0, rank), :] = exact_across(mid, exact(proj, lower))
        for k in range(3):
            rest[pl.ds((k + 1) * rank, rank), :] = part[3 + k]

    square = (rank, rank)
    return small(kernel, flags, (own, other), (square, square, (4 * rank, rank)), flops=10**9)


def group_matrices(flags, own, other):
    rank = own.shape[1]

    def kernel(f, x, y, sys_inverse, down, rest):
        part = [x[pl.ds(k * rank, rank), :] + y[pl.ds(k * rank, rank), :] for k in range(4)]
        proj, coup, top, root = part
        inv = inverse(proj + coup)
        sys_inverse[...] = inv
        lower = exact(exact(inv, coup), top)
        down[...] = lower
        rest[...] = root + exact_across(top, exact(proj, lower))

    square = (rank, rank)
    return small(kernel, flags, (own, other), (square, square, square), flops=10**9)


def root_inverse(flags, own, other):
    def kernel(f, x, y, out):
        out[...] = inverse(x[...] + y[...])

    return small(kernel, flags, (own, other), (own.shape,), flops=10**9)[0]


def near_inner(flags, base, diagonal, lower, upper, value, beside, weights=None):
    rows, rhs = value.shape

    def kernel(f, r, d, lo, up, v, w, *rest):
        if weights is not None:
            far_lo, far_up, near_w, own_w, far_w, out, coupled, vh, vl, wh, wl, sc = rest
        else:
            out, vh, vl, wh, wl = rest

        @pl.when(pl.program_id(0) == 0)
        def _():
            vh[...], vl[...] = split(v[...])
            wh[...], wl[...] = split(w[...])
            if weights is not None:
                for k, ref in enumerate((own_w, near_w, far_w)):
                    sc[2 * k], sc[2 * k + 1] = split(ref[...])

        def run(near, far):
            dd = split(d[...])
            nn = split(near[...])
            out[...] = r[...] - (mul(dd, (vh[...], vl[...])) + mul(nn, (wh[...], wl[...])))
            if weights is not None:
                rank = own_w.shape[1]
                coupled[:, pl.ds(0, rank)] = mul(dd, (sc[0], sc[1])) + mul(nn, (sc[2], sc[3]))
                coupled[:, pl.ds(rank, rank)] = mul(split(far[...]), (sc[4], sc[5]))

        @pl.when(f[0] == 0)
        def _():
            run(up, far_lo if weights is not None else None)

        @pl.when(f[0] == 1)
        def _():
            run(lo, far_up if weights is not None else None)

    even = pl.BlockSpec((ROWS, rows), lambda s, f: (s * (1 - f[0]), 0))
    odd = pl.BlockSpec((ROWS, rows), lambda s, f: (s * f[0], 0))
    operands = [base, diagonal, lower, upper, value, beside]
    specs = [strip(rhs), strip(rows), odd, even, whole((rows, rhs)), whole((rows, rhs))]
    outs = [jax.ShapeDtypeStruct((rows, rhs), f32)]
    out_specs = [strip(rhs)]
    scratch = [pltpu.VMEM((rows, rhs), bf16) for _ in range(4)]
    flops = 3 * 2 * 2 * rows * rows * rhs
    if weights is not None:
        stack_other, own, far = weights
        rank = own.shape[1]
        operands += [lower, upper, stack_other, own, far]
        specs += [even, odd, whole((rows, rank)), whole((rows, rank)), whole((rows, rank))]
        outs.append(jax.ShapeDtypeStruct((rows, 2 * rank), f32))
        out_specs.append(strip(2 * rank))
        scratch.append(pltpu.VMEM((6, rows, rank), bf16))
        flops += 3 * 3 * 2 * rows * rows * rank
    return call(
        kernel, flags, operands, specs, outs, out_specs, (rows // ROWS,), scratch, flops
    )


def residual_terms(flags, base, lower, upper, far, weight):
    rows, rhs = base.shape
    rank = weight.shape[1]
    half = rhs // 2

    def kernel(f, r, lo, up, v, w, out, keep, send, vh, vl, total):
        step = pl.program_id(0)

        @pl.when(step == 0)
        def _():
            vh[...], vl[...] = split(v[...])
            total[...] = jnp.zeros_like(total)

        def run(near):
            value = r[...] - mul(split(near[...]), (vh[...], vl[...]))
            out[...] = value
            total[...] += mul_across(split(w[...]), split(value))

        @pl.when(f[0] == 0)
        def _():
            run(lo)

        @pl.when(f[0] == 1)
        def _():
            run(up)

        @pl.when(step == pl.num_programs(0) - 1)
        def _():
            keep[...] = total[:, pl.ds(pl.multiple_of(f[0] * half, half), half)]
            send[...] = total[:, pl.ds(pl.multiple_of((1 - f[0]) * half, half), half)]

    even = pl.BlockSpec((ROWS, rows), lambda s, f: (s * (1 - f[0]), 0))
    odd = pl.BlockSpec((ROWS, rows), lambda s, f: (s * f[0], 0))
    return call(
        kernel,
        flags,
        (base, lower, upper, far, weight),
        [strip(rhs), even, odd, whole((rows, rhs)), strip(rank)],
        [jax.ShapeDtypeStruct(shape, f32) for shape in ((rows, rhs), (rank, half), (rank, half))],
        [strip(rhs), whole((rank, half)), whole((rank, half))],
        (rows // ROWS,),
        [pltpu.VMEM((rows, rhs), bf16), pltpu.VMEM((rows, rhs), bf16), pltpu.VMEM((rank, rhs), f32)],
        3 * 2 * rows * rows * rhs,
    )


def local_update(flags, guess, inverse_block, residual):
    rows, rhs = guess.shape

    def kernel(f, g, a, r, out, rh, rl):
        @pl.when(pl.program_id(0) == 0)
        def _():
            rh[...], rl[...] = split(r[...])

        out[...] = g[...] + mul(split(a[...]), (rh[...], rl[...]))

    return call(
        kernel,
        flags,
        (guess, inverse_block, residual),
        [strip(rhs), strip(rows), whole((rows, rhs))],
        [jax.ShapeDtypeStruct((rows, rhs), f32)],
        [strip(rhs)],
        (rows // ROWS,),
        [pltpu.VMEM((rows, rhs), bf16), pltpu.VMEM((rows, rhs), bf16)],
        3 * 2 * rows * rows * rhs,
    )[0]


def finish(flags, partial, lower, upper, far, coupled, inner, outer, update, weight):
    rows, rhs = partial.shape
    rank = weight.shape[1]

    def kernel(f, z, lo, up, v, g, bi, bo, y, w, fresh, out, vh, vl, ch, cl):
        @pl.when(pl.program_id(0) == 0)
        def _():
            vh[...], vl[...] = split(v[...])
            ch[pl.ds(0, rank), :], cl[pl.ds(0, rank), :] = split(bi[...])
            crossing = f[0] == f[1]
            ch[pl.ds(rank, rank), :], cl[pl.ds(rank, rank), :] = split(
                jnp.where(crossing, bo[...], bi[...])
            )

        both = (ch[...], cl[...])
        own = (ch[pl.ds(0, rank), :], cl[pl.ds(0, rank), :])
        fresh[...] = y[...] - mul(split(w[...]), own)
        rest = z[...] + mul(split(g[...]), both)

        @pl.when(f[0] == 0)
        def _():
            out[...] = rest - mul(split(lo[...]), (vh[...], vl[...]))

        @pl.when(f[0] == 1)
        def _():
            out[...] = rest - mul(split(up[...]), (vh[...], vl[...]))

    even = pl.BlockSpec((ROWS, rows), lambda s, f: (s * (1 - f[0]), 0))
    odd = pl.BlockSpec((ROWS, rows), lambda s, f: (s * f[0], 0))
    field = jax.ShapeDtypeStruct((rows, rhs), f32)
    return call(
        kernel,
        flags,
        (partial, lower, upper, far, coupled, inner, outer, update, weight),
        [
            strip(rhs),
            even,
            odd,
            whole((rows, rhs)),
            strip(2 * rank),
            whole((rank, rhs)),
            whole((rank, rhs)),
            strip(rhs),
            strip(rank),
        ],
        [field, field],
        [strip(rhs), strip(rhs)],
        (rows // ROWS,),
        [pltpu.VMEM((rows, rhs), bf16) for _ in range(2)]
        + [pltpu.VMEM((2 * rank, rhs), bf16) for _ in range(2)],
        3 * 2 * rows * (rows + 3 * rank) * rhs,
    )


def fold(flags, keep, received, bit):
    rank, width = keep.shape
    half = width // 2

    def kernel(f, x, y, kept, sent, total):
        total[...] = x[...] + y[...]
        kept[...] = total[:, pl.ds(pl.multiple_of(f[bit] * half, half), half)]
        sent[...] = total[:, pl.ds(pl.multiple_of((1 - f[bit]) * half, half), half)]

    shape = jax.ShapeDtypeStruct((rank, half), f32)
    return call(
        kernel,
        flags,
        (keep, received),
        [whole((rank, width))] * 2,
        [shape, shape],
        [whole((rank, half))] * 2,
        scratch=[pltpu.VMEM((rank, width), f32)],
    )


def lift(flags, own, other, down):
    def kernel(f, x, y, k, total, up):
        value = x[...] + y[...]
        total[...] = value
        up[...] = exact_across(k[...], value)

    return small(kernel, flags, (own, other, down), (own.shape, (down.shape[1], own.shape[1])))


def descend(flags, own, other, root_inv, group_down, group_inv, group_rhs, down, inv, block_rhs):
    def kernel(f, x, y, ri, gd, gi, gr, d, i, br, out):
        root = exact(ri[...], x[...] + y[...])
        group = exact(gd[...], root) + exact(gi[...], gr[...])
        out[...] = exact(d[...], group) + exact(i[...], br[...])

    operands = (own, other, root_inv, group_down, group_inv, group_rhs, down, inv, block_rhs)
    return small(kernel, flags, operands, (own.shape,))[0]


def place(flags, own, other, bit):
    rank, width = own.shape

    def kernel(f, x, y, out):
        out[:, pl.ds(pl.multiple_of(f[bit] * width, width), width)] = x[...]
        out[:, pl.ds(pl.multiple_of((1 - f[bit]) * width, width), width)] = y[...]

    return small(kernel, flags, (own, other), ((rank, 2 * width),))[0]


def body(
    right_side,
    guess,
    near_diag,
    near_lower,
    near_upper,
    leaf_inverse,
    leaf_basis,
    leaf_transfer,
    mid_share,
    top_share,
    coupling_share,
):
    groups, leaves = lax.axis_size("grp"), lax.axis_size("leaf")
    total = groups * leaves
    diagonal, lower, upper = near_diag[0], near_lower[0], near_upper[0]
    inverse_block = leaf_inverse[0]
    rows, rank = leaf_basis.shape[1:]

    def swap(value, axis, mask):
        size = lax.axis_size(axis)
        return lax.ppermute(value, axis, [(i, i ^ mask) for i in range(size)])

    def swap_off_chip(value, stride=2):
        pairs = []
        for i in range(stride, total, stride):
            pairs += [(i - 1, i), (i, i - 1)]
        return lax.ppermute(value, AXES, pairs)

    def bits(count, first=1):
        masks = []
        while first < count:
            masks.append(first)
            first *= 2
        return masks

    index = lax.axis_index("leaf")
    flags = jnp.stack([index % 2, index // 2 % 2]).astype(jnp.int32)

    guess_far = swap_off_chip(guess)
    guess_beside = swap(guess, "leaf", 1)

    stack, weight = leaf_setup(
        flags, inverse_block, leaf_basis[0], leaf_transfer[0], mid_share[0], top_share[0], coupling_share[0]
    )
    stack_beside = swap(stack, "leaf", 1)
    pair = stack[rows:] + stack_beside[rows:]
    block_inv, block_down, rest = block_matrices(flags, pair, swap(pair, "leaf", 2))
    masks = bits(leaves, NODE)
    for mask in masks[:-1]:
        rest = rest + swap(rest, "leaf", mask)
    group_inv, group_down, rest = group_matrices(flags, rest, swap(rest, "leaf", masks[-1]))
    for mask in bits(groups)[:-1]:
        rest = rest + swap(rest, "grp", mask)
    root_inv = root_inverse(flags, rest, swap(rest, "grp", bits(groups)[-1]))

    (partial,) = near_inner(flags, right_side, diagonal, lower, upper, guess, guess_beside)
    residual, keep, send = residual_terms(flags, partial, lower, upper, guess_far, weight)
    weight_ready, _ = lax.optimization_barrier((weight, guess_far))
    weight_far = swap_off_chip(weight_ready)
    update = local_update(flags, guess, inverse_block, residual)
    update_far = swap_off_chip(update)
    update_beside = swap(update, "leaf", 1)

    keep, send = fold(flags, keep, swap(send, "leaf", 1), 1)
    block_rhs, rhs = lift(flags, keep, swap(send, "leaf", 2), block_down)
    for mask in masks[:-1]:
        rhs = rhs + swap(rhs, "leaf", mask)
    group_rhs, rhs = lift(flags, rhs, swap(rhs, "leaf", masks[-1]), group_down)
    for mask in bits(groups)[:-1]:
        rhs = rhs + swap(rhs, "grp", mask)
    out = descend(
        flags, rhs, swap(rhs, "grp", bits(groups)[-1]),
        root_inv, group_down, group_inv, group_rhs, block_down, block_inv, block_rhs,
    )
    out = place(flags, out, swap(out, "leaf", 2), 1)
    out = place(flags, out, swap(out, "leaf", 1), 0)
    out_far = swap_off_chip(out, NODE)

    partial, coupled = near_inner(
        flags, right_side, diagonal, lower, upper, update, update_beside,
        (stack_beside, weight, weight_far),
    )
    return tuple(
        finish(flags, partial, lower, upper, update_far, coupled, out, out_far, update, weight)
    )


def solution(mesh):
    leaf = P(AXES, None, None)
    in_specs = (P(AXES, None), P(AXES, None)) + (leaf,) * 8 + (P(AXES, None, None, None),)
    out_specs = (P(AXES, None), P(AXES, None))
    return jax.shard_map(body, mesh=mesh, in_specs=in_specs, out_specs=out_specs, check_vma=False)
```
